32 devices in a mesh: ab: 2 (over y), cd: 16 (over z, x, core).
Axes of the slice: x: 2, y: 2, z: 4, core: 2. Of those that a mesh axis runs over, the one named last changes fastest.
Arguments:
- amplitudes: float32 [768, 16384], P('cd', 'ab'), may hold values from -1.25 to 1.25
- driver: float32 [768, 16384], P('cd', 'ab'), may hold values from -6 to 6
- ladder: bfloat16 [16384, 16384], P('ab', 'cd'), may hold values from -0.125 to 0.125
- block_mask: int32 [128, 128], P('ab', 'cd'), may hold values 0 or 1
- pair_list: int32 [768], replicated, may hold values from 0 to 1023, as said below
- occ_energy: float32 [32], replicated, may hold values from -2 to -0.5
- virt_energy: float32 [128], replicated, may hold values from 0.5 to 3
Outputs:
- new_amplitudes: float32 [768, 16384], P('cd', 'ab')
The draws below stay inside these ranges and needn't reach their ends.
Inputs may be any that keep to these rules, and one draw needn't show every extreme that they name: `pair_list`: the entries are distinct occupied pairs i * 32 + j. Rows come in aligned blocks of two: a pair with i != j shares its block with the pair (j, i); pairs with i == j stand two to a block. Pairs 0 and 1023 are always listed.
All inputs are finite; a program needn't handle non-finite values. No bound on the sum of `block_mask` on one device may be relied on, other than what follows from the above.
Results may differ from the reference program's by a relative error of at most 0.008.
Values may be sent and summed in bfloat16 or wider, within the bound.
A program may use at most 128 MiB of HBM per device.

```python
import jax
import jax.numpy as jnp
import numpy as np
from jax import lax

NV = 128
NOCC = 32
M_PAIRS = 768
BLK = 128
ITERS = 2
NP = 16384
N_AB = 2
N_CD = 16


def draw_pair_list(key, part):
    upper_i, upper_j = np.triu_indices(NOCC, 1)
    diag_even = np.arange(0, NOCC, 2)
    diag_odd = np.arange(1, NOCC, 2)
    lead = np.concatenate([upper_i * NOCC + upper_j, diag_even * NOCC + diag_even]).astype(np.int32)
    trail = np.concatenate([upper_j * NOCC + upper_i, diag_odd * NOCC + diag_odd]).astype(np.int32)
    units = lead.shape[0]
    forced = np.zeros((units,), np.int32)
    forced[units - NOCC // 2] = 1
    forced[units - 1] = 1
    lead_table = jnp.asarray(lead)
    trail_table = jnp.asarray(trail)
    scores = jax.random.randint(jax.random.fold_in(key, 11), (units,), 0, 1 << 16)
    scores = (scores + jnp.asarray(forced) * (1 << 17)) * units + jnp.arange(units, dtype=jnp.int32)
    chosen = lax_top(scores, M_PAIRS // 2)
    shuffle = jax.random.permutation(jax.random.fold_in(key, 12), M_PAIRS // 2)
    chosen = chosen[shuffle]
    turn = jax.random.randint(jax.random.fold_in(key, 13), (M_PAIRS // 2,), 0, 2)
    head = jnp.where(turn == 1, trail_table[chosen], lead_table[chosen])
    tail = jnp.where(turn == 1, lead_table[chosen], trail_table[chosen])
    return jnp.stack([head, tail], axis=1).reshape(M_PAIRS).astype(jnp.int32)


def lax_top(scores, count):
    values, indices = jax.lax.top_k(scores, count)
    return indices.astype(jnp.int32)


def touch_ends(entries, key, smallest, largest):
    extent = entries.shape
    index_at = [jax.random.randint(jax.random.fold_in(key, axis), (), 0, extent[axis]) for axis in range(len(extent))]
    entries = entries.at[tuple(index_at)].set(smallest)
    longest = extent.index(max(extent))
    index_at[longest] = (index_at[longest] + 1) % extent[longest]
    return entries.at[tuple(index_at)].set(largest)


def shard_levels(stream_key, dims, cuts, smallest, high):
    gain = 1.0
    for dim, blocks in cuts:
        heights = jax.random.uniform(jax.random.fold_in(jax.random.fold_in(stream_key, 6), dim), (blocks,), jnp.float32, smallest / len(cuts), high / len(cuts))
        gain = gain * jnp.repeat(jnp.exp(heights), dims[dim] // blocks).reshape((-1,) + (1,) * (len(dims) - 1 - dim))
    return gain


def gaussian(key, extent, deviation, reach, cuts=(), held_as=jnp.bfloat16):
    values = deviation * jax.random.normal(key, extent, jnp.float32)
    if cuts:
        values = values * shard_levels(key, extent, cuts, -0.22, 0.18)
    return jnp.clip(values, -reach, reach).astype(held_as)


def setup_inputs(seed: int = 0) -> dict:
    seeds = jax.random.split(jax.random.key(seed), 8)
    amplitudes = gaussian(seeds[0], (M_PAIRS, NP), 0.2, 1.25, ((0, 16), (1, 2)), jnp.float32)
    driver = gaussian(seeds[1], (M_PAIRS, NP), 1.0, 6.0, ((0, 16), (1, 2)), jnp.float32)
    ladder = gaussian(seeds[2], (NP, NP), (NP // 8) ** -0.5, 0.125, ((0, 2), (1, 16)))
    block_mask = touch_ends((jax.random.randint(seeds[3], (NP // BLK, NP // BLK), 0, 100) < 37).astype(jnp.int32), jax.random.fold_in(seeds[3], 1), 0, 1)
    pair_list = draw_pair_list(jax.random.fold_in(seeds[7], 71), 0)
    occ_energy = jnp.clip(jax.random.uniform(seeds[5], (NOCC,), jnp.float32, -2.0, -0.5), -2.0, -0.5)
    virt_energy = jnp.clip(jax.random.uniform(seeds[6], (NV,), jnp.float32, 0.5, 3.0), 0.5, 3.0)
    return {"amplitudes": amplitudes, "driver": driver, "ladder": ladder, "block_mask": block_mask, "pair_list": pair_list, "occ_energy": occ_energy, "virt_energy": virt_energy}


def pair_maps():
    tile = NV // N_AB
    pairs = jnp.arange(NP, dtype=jnp.int32)
    big_a = pairs // (tile * NV)
    big_b = (pairs // (tile * tile)) % N_AB
    inner_a = (pairs // tile) % tile
    inner_b = pairs % tile
    first = big_a * tile + inner_a
    second = big_b * tile + inner_b
    mirror = big_b * (tile * NV) + big_a * (tile * tile) + inner_b * tile + inner_a
    in_block = NP // N_CD
    piece = NP // (N_AB * N_CD)
    slot = pairs // in_block
    source = (pairs % in_block) // piece
    rest = pairs % piece
    position = source * (NP // N_AB) + slot * piece + rest
    return first, second, mirror, position


def reference(amplitudes, driver, ladder, block_mask, pair_list, occ_energy, virt_energy):
    first, second, mirror, position = pair_maps()
    occ_i = pair_list // NOCC
    occ_j = pair_list % NOCC
    denominator = (virt_energy[first] + virt_energy[second])[None, :] - (occ_energy[occ_i] + occ_energy[occ_j])[:, None]
    inverse = jnp.zeros((NOCC * NOCC,), jnp.int32).at[pair_list].set(jnp.arange(M_PAIRS, dtype=jnp.int32))
    mirror_row = inverse[occ_j * NOCC + occ_i]
    out_block = NP // N_AB
    in_block = NP // N_CD
    ladder_rows = ladder.reshape(N_AB, out_block, NP)
    mask_rows = block_mask.reshape(N_AB, out_block // BLK, NP // BLK)
    state = amplitudes
    for step in range(ITERS):
        low = state.astype(jnp.bfloat16)[:, position].astype(jnp.float32)

        def block_product(operands):
            rows_here, mask_here = operands
            masked = rows_here.astype(jnp.float32).reshape(out_block // BLK, BLK, NP // BLK, BLK)
            masked = masked * mask_here.astype(jnp.float32)[:, None, :, None]
            masked = masked.reshape(out_block, NP)

            def one_block(carry, index):
                start = index * in_block
                left = lax.dynamic_slice_in_dim(low, start, in_block, 1)
                right = lax.dynamic_slice_in_dim(masked, start, in_block, 1)
                part = jnp.dot(left, right.T, precision=lax.Precision.HIGHEST)
                return carry + part.astype(jnp.bfloat16).astype(jnp.float32), None

            zeros = jnp.zeros((M_PAIRS, out_block), jnp.float32)
            total, unused = lax.scan(one_block, zeros, jnp.arange(N_CD, dtype=jnp.int32))
            return total

        blocks = lax.map(block_product, (ladder_rows, mask_rows))
        ladder_term = jnp.transpose(blocks, (1, 0, 2)).reshape(M_PAIRS, NP)
        symmetric = ladder_term + ladder_term[mirror_row][:, mirror]
        state = (driver + symmetric) / denominator
    return state
```

```python
import jax
import jax.numpy as jnp
from jax import lax
from jax.sharding import PartitionSpec as P

NV = 128
NOCC = 32
BLK = 128
ITERS = 2


def flip_tiles(tiles, tile_width):
    row_count, tile_count = tiles.shape[:2]
    turned = jnp.swapaxes(tiles.reshape(row_count, tile_count, tile_width, tile_width), 2, 3)
    return turned.reshape(row_count, tile_count * tile_width * tile_width)


def body(amplitudes, driver, ladder, block_mask, pair_list, occ_energy, virt_energy):
    ab_count = lax.axis_size("ab")
    ab_index = lax.axis_index("ab")
    cd_index = lax.axis_index("cd")
    rows_dev, cols_dev = amplitudes.shape
    out_rows, in_cols = ladder.shape
    tile_width = NV // ab_count
    tile_area = tile_width * tile_width
    weights = ladder.reshape(out_rows // BLK, BLK, in_cols // BLK, BLK)
    weights = (weights * block_mask.astype(jnp.bfloat16)[:, None, :, None]).reshape(
        out_rows, in_cols
    )
    pairs_local = ab_index * cols_dev + jnp.arange(cols_dev, dtype=jnp.int32)
    big_a = pairs_local // (tile_width * NV)
    big_b = pairs_local // tile_area % ab_count
    first = big_a * tile_width + pairs_local // tile_width % tile_width
    second = big_b * tile_width + pairs_local % tile_width
    virt_index = jnp.arange(NV, dtype=jnp.int32)
    picks = (first[:, None] == virt_index).astype(jnp.float32) + (
        second[:, None] == virt_index
    ).astype(jnp.float32)
    col_energy = jnp.dot(picks, virt_energy, precision=lax.Precision.HIGHEST)
    row_pairs = lax.dynamic_slice_in_dim(pair_list, cd_index * rows_dev, rows_dev)
    occ_index = jnp.arange(NOCC, dtype=jnp.int32)
    occ_picks = (row_pairs[:, None] // NOCC == occ_index).astype(jnp.float32)
    occ_picks = occ_picks + (row_pairs[:, None] % NOCC == occ_index).astype(jnp.float32)
    row_energy = jnp.dot(occ_picks, occ_energy, precision=lax.Precision.HIGHEST)
    denominator = col_energy[None, :] - row_energy[:, None]
    local_diagonal = row_pairs // NOCC == row_pairs % NOCC
    row_index = jnp.arange(rows_dev, dtype=jnp.int32)
    mirror_row = jnp.where(local_diagonal, row_index, row_index ^ 1)
    row_swap = (mirror_row[:, None] == row_index).astype(jnp.bfloat16)
    state = amplitudes
    for step in range(ITERS):
        rounded = state.astype(jnp.bfloat16)
        regrouped = lax.all_to_all(rounded, "cd", split_axis=1, concat_axis=0, tiled=True)
        partial_value = lax.dot_general(
            lax.all_gather(regrouped, "ab", axis=1, tiled=True),
            weights,
            (((1,), (1,)), ((), ())),
            preferred_element_type=jnp.float32,
        )
        received = lax.psum_scatter(
            partial_value.astype(jnp.bfloat16), "cd", scatter_dimension=0, tiled=True
        )
        swapped = jnp.dot(row_swap, received, preferred_element_type=jnp.float32)
        tiles = lax.all_to_all(
            swapped.astype(jnp.bfloat16).reshape(rows_dev, ab_count, tile_area),
            "ab",
            split_axis=1,
            concat_axis=1,
            tiled=True,
        )
        symmetric = received.astype(jnp.float32) + flip_tiles(tiles, tile_width).astype(jnp.float32)
        state = (driver + symmetric) / denominator
    return state


def solution(mesh):
    placed = (P("cd", "ab"), P("cd", "ab"), P("ab", "cd"), P("ab", "cd"), P(), P(), P())
    return jax.shard_map(body, mesh=mesh, in_specs=placed, out_specs=P("cd", "ab"), check_vma=False)
```

```python
import jax
import jax.numpy as jnp
from jax import lax
from jax.sharding import PartitionSpec as P

NV = 128
NOCC = 32
BLK = 128
ITERS = 2
CORES = 2
CHUNKS = 2


def flip_tiles(tiles, tile_width):
    row_count, tile_count = tiles.shape[:2]
    turned = jnp.swapaxes(tiles.reshape(row_count, tile_count, tile_width, tile_width), 2, 3)
    return turned.reshape(row_count, tile_count * tile_width * tile_width)


def product(rows, weight):
    flat = rows.reshape(-1, rows.shape[-1])
    return lax.dot_general(
        flat, weight, (((1,), (1,)), ((), ())), preferred_element_type=jnp.float32
    ).astype(jnp.bfloat16)


def body(amplitudes, driver, ladder, block_mask, pair_list, occ_energy, virt_energy):
    ab_count = lax.axis_size("ab")
    ab_index = lax.axis_index("ab")
    cd_index = lax.axis_index("cd")
    rows_dev, cols_dev = amplitudes.shape
    out_rows, in_cols = ladder.shape
    tile_width = NV // ab_count
    tile_area = tile_width * tile_width
    weights = ladder.reshape(out_rows // BLK, BLK, in_cols // BLK, BLK)
    weights = (weights * block_mask.astype(jnp.bfloat16)[:, None, :, None]).reshape(
        out_rows, in_cols
    )
    pairs_local = ab_index * cols_dev + jnp.arange(cols_dev, dtype=jnp.int32)
    big_a = pairs_local // (tile_width * NV)
    big_b = pairs_local // tile_area % ab_count
    first = big_a * tile_width + pairs_local // tile_width % tile_width
    second = big_b * tile_width + pairs_local % tile_width
    virt_index = jnp.arange(NV, dtype=jnp.int32)
    picks = (first[:, None] == virt_index).astype(jnp.float32) + (
        second[:, None] == virt_index
    ).astype(jnp.float32)
    col_energy = jnp.dot(picks, virt_energy, precision=lax.Precision.HIGHEST)
    row_pairs = lax.dynamic_slice_in_dim(pair_list, cd_index * rows_dev, rows_dev)
    occ_index = jnp.arange(NOCC, dtype=jnp.int32)
    occ_picks = (row_pairs[:, None] // NOCC == occ_index).astype(jnp.float32)
    occ_picks = occ_picks + (row_pairs[:, None] % NOCC == occ_index).astype(jnp.float32)
    row_energy = jnp.dot(occ_picks, occ_energy, precision=lax.Precision.HIGHEST)
    denominator = col_energy[None, :] - row_energy[:, None]
    local_diagonal = row_pairs // NOCC == row_pairs % NOCC
    row_index = jnp.arange(rows_dev, dtype=jnp.int32)
    mirror_row = jnp.where(local_diagonal, row_index, row_index ^ 1)
    row_swap = (mirror_row[:, None] == row_index).astype(jnp.bfloat16)
    cd_count = lax.axis_size("cd")
    core = cd_index % CORES
    core_swap = [(index, index ^ 1) for index in range(cd_count)]
    core_groups = [list(range(start, cd_count, CORES)) for start in range(CORES)]
    chunk_rows = out_rows // CHUNKS
    state = amplitudes
    for step in range(ITERS):
        rounded = state.astype(jnp.bfloat16)
        regrouped = lax.all_to_all(rounded, "cd", split_axis=1, concat_axis=0, tiled=True)
        gathered = lax.all_gather(regrouped, "ab", axis=1, tiled=True)
        by_core = gathered.reshape(cd_count // CORES, CORES, rows_dev, in_cols)
        other_rows = lax.dynamic_index_in_dim(by_core, 1 - core, 1, keepdims=False)
        own_rows = lax.dynamic_index_in_dim(by_core, core, 1, keepdims=False)
        pieces = []
        for chunk in range(CHUNKS):
            weight = weights[chunk * chunk_rows : (chunk + 1) * chunk_rows]
            sent = lax.ppermute(product(other_rows, weight), "cd", core_swap)
            kept = product(own_rows, weight)
            both = (sent.astype(jnp.float32) + kept.astype(jnp.float32)).astype(jnp.bfloat16)
            pieces.append(
                lax.psum_scatter(
                    both, "cd", scatter_dimension=0, axis_index_groups=core_groups, tiled=True
                )
            )
        received = jnp.concatenate(pieces, axis=1)
        swapped = jnp.dot(row_swap, received, preferred_element_type=jnp.float32)
        tiles = lax.all_to_all(
            swapped.astype(jnp.bfloat16).reshape(rows_dev, ab_count, tile_area),
            "ab",
            split_axis=1,
            concat_axis=1,
            tiled=True,
        )
        symmetric = received.astype(jnp.float32) + flip_tiles(tiles, tile_width).astype(jnp.float32)
        state = (driver + symmetric) / denominator
    return state


def solution(mesh):
    placed = (P("cd", "ab"), P("cd", "ab"), P("ab", "cd"), P("ab", "cd"), P(), P(), P())
    return jax.shard_map(body, mesh=mesh, in_specs=placed, out_specs=P("cd", "ab"), check_vma=False)
```
